512 devices in a mesh: tile: 16 (over z_lo, x, core), kern: 32 (over z_hi, y).
Axes of the slice: x: 4, y: 8, z: 8 (z_hi: 4, z_lo: 2; z = z_hi * 2 + z_lo), core: 2. Of those that a mesh axis runs over, the one named last changes fastest.
Arguments:
- mask: float32 [1024, 2048], P('tile'), may hold values from 0 to 1
- target: int32 [1024, 2048], P('tile'), may hold values 0 or 1
- kernels: bfloat16 [32, 2, 21, 21], P('kern'), may hold values from -0.25 to 0.25
- source_weight: float32 [32], replicated, may hold values from 0.2 to 2
- assign: int32 [32], P('kern'), may hold values from 0 to 31, each once
Outputs:
- mask_grad: float32 [1024, 2048], P('tile', 'kern')
- resist: float32 [1024, 2048], P('tile', 'kern')
The draws below stay inside these ranges and needn't reach their ends.
Inputs may be any that keep to these rules, and one draw needn't show every extreme that they name: assign is a permutation of 0 to 31.
All inputs are finite; a program needn't handle non-finite values. No bound on the sum of `target` on one device may be relied on, other than what follows from the above.
Results may differ from the reference program's by a relative error of at most 0.0036.
Values may be sent and summed in bfloat16 or wider, within the bound.
No kernel may reach another device: no remote copies, remote signals or barrier semaphores. Data moves between devices by JAX's collectives and lax.ppermute only.
A program may use at most 64 MiB of HBM per device.

```python
import math
import jax
import jax.numpy as jnp
from jax import lax

KS = 21
COLS = 2048
SOURCES = 32
ROWS = 1024


def with_ends(drawn, rng, low, largest):
    index_at = [jax.random.randint(jax.random.fold_in(rng, axis), (), 0, length) for axis, length in enumerate(drawn.shape)]
    main_axis = drawn.shape.index(max(drawn.shape))
    next_to = index_at[:main_axis] + [(index_at[main_axis] + 1) % drawn.shape[main_axis]] + index_at[main_axis + 1:]
    return drawn.at[tuple(index_at)].set(low).at[tuple(next_to)].set(largest)


def shard_levels(key, extent, pieces, low, largest):
    factor_of, own = 1.0, jax.random.fold_in(key, 6)
    for dim, parts in pieces:
        steps = jnp.exp(jax.random.uniform(jax.random.fold_in(own, dim), (parts,), jnp.float32, low / len(pieces), largest / len(pieces)))
        factor_of = factor_of * jnp.repeat(steps, extent[dim] // parts).reshape([-1 if axis == dim else 1 for axis in range(len(extent))])
    return factor_of


def scatter_about(stream_key, dims, spread, bound, pieces=(), held_as=jnp.bfloat16):
    level = shard_levels(stream_key, dims, pieces, -0.22, 0.18) if pieces else 1.0
    entries = jax.random.normal(stream_key, dims, jnp.float32) * spread * level
    return jnp.minimum(jnp.maximum(entries, -bound), bound).astype(held_as)


def setup_inputs(seed: int = 0) -> dict:
    streams_of = jax.random.split(jax.random.key(seed), 6)
    return {
        "mask": jnp.clip(1.0 * jax.random.uniform(streams_of[0], (ROWS, COLS), jnp.float32) ** shard_levels(streams_of[0], (ROWS, COLS), ((0, 16),), -0.2, 0.2), 0.0, 1.0),
        "target": with_ends((jax.random.randint(streams_of[1], (ROWS, COLS), 0, 2) < 1).astype(jnp.int32), jax.random.fold_in(streams_of[1], 1), 0, 1),
        "kernels": scatter_about(streams_of[2], (SOURCES, 2, KS, KS), (KS * KS) ** -0.5, 0.25, ((0, 32),)),
        "source_weight": jnp.clip(jnp.exp(jax.random.uniform(streams_of[3], (SOURCES,), jnp.float32, math.log(0.2), math.log(2.0))), 0.2, 2.0),
        "assign": jax.random.permutation(streams_of[4], SOURCES).astype(jnp.int32),
    }


def reference(mask, target, kernels, source_weight, assign):
    margin = (KS - 1) // 2
    copy_wide = mask.astype(jnp.bfloat16).astype(jnp.float32)
    weights = jnp.take(source_weight, assign.astype(jnp.int32))
    total = jnp.sum(source_weight)

    def fields_of(kernel_pair):
        rhs = kernel_pair.astype(jnp.float32)[:, None]
        out = lax.conv_general_dilated(copy_wide[None, None], rhs, (1, 1), ((margin, margin), (margin, margin)), precision=lax.Precision.HIGHEST)
        return out[0]

    def add_image(carry, packed):
        kernel_pair, weight_one = packed
        fields = fields_of(kernel_pair)
        return (carry + weight_one * (fields[0] * fields[0] + fields[1] * fields[1]), None)
    aerial, unused = lax.scan(add_image, jnp.zeros(mask.shape, jnp.float32), (kernels, weights))
    aerial = aerial / total
    resist = jax.nn.sigmoid(4.0 * (aerial - 0.6))
    sense = 2.0 * (resist - target.astype(jnp.float32)) * 4.0 * resist * (1.0 - resist)

    def add_grad(carry, packed):
        kernel_pair, weight_one = packed
        fields = fields_of(kernel_pair)
        adjoint = (2.0 * weight_one / total * sense[None] * fields).astype(jnp.bfloat16).astype(jnp.float32)
        flipped = kernel_pair[:, ::-1, ::-1].astype(jnp.float32)[None]
        out = lax.conv_general_dilated(adjoint[None], flipped, (1, 1), ((margin, margin), (margin, margin)), precision=lax.Precision.HIGHEST)
        return (carry + out[0, 0], None)
    mask_grad, unused_two = lax.scan(add_grad, jnp.zeros(mask.shape, jnp.float32), (kernels, weights))
    return (mask_grad, resist)
```

```python
import jax
import jax.numpy as jnp
from jax import lax
from jax.experimental import pallas as pl
from jax.experimental.pallas import tpu as pltpu
from jax.sharding import PartitionSpec as P

OWN = 64
SPAN = 21
HALF = 10
SOURCES = 32
CHANNELS = 2 * SOURCES
DEPTH = 24
TAPS = 512
WEIGHT_SLOT = SPAN * DEPTH
CHUNKS = 11
SLOPE = 4.0
LEVEL = 0.6
VMEM = pltpu.VMEM


def pack_kernel(assign_ref, taps_ref, weight_ref, out_ref):
    slot = lax.broadcasted_iota(jnp.int32, (SPAN, TAPS), 1)
    row = lax.broadcasted_iota(jnp.int32, (SPAN, TAPS), 0)
    low = DEPTH * row
    spread = ((slot >= low) & (slot < low + DEPTH)).astype(jnp.float32).astype(jnp.bfloat16)
    place = slot.astype(jnp.float32)
    inner = place - DEPTH * jnp.floor((place + 0.5) * (1.0 / DEPTH))
    keep = inner == row.astype(jnp.float32)
    index = lax.broadcasted_iota(jnp.int32, (1, SOURCES), 1)
    weight = jnp.sum(jnp.where(index == assign_ref[0], weight_ref[...], 0.0), axis=1, keepdims=True)
    lane = lax.broadcasted_iota(jnp.int32, (1, TAPS), 1)
    rows = []
    for part in range(2):
        wide = jnp.dot(taps_ref[part], spread, preferred_element_type=jnp.float32)
        flat = jnp.sum(jnp.where(keep, wide, 0.0), axis=0, keepdims=True)
        flat = jnp.where(lane == WEIGHT_SLOT, weight, flat)
        rows += [flat[:, 128 * q : 128 * q + 128] for q in range(4)]
    out_ref[...] = jnp.broadcast_to(jnp.concatenate(rows, axis=0)[None], out_ref.shape)


def pack(assign, kernels, source_weight):
    return pl.pallas_call(
        pack_kernel,
        out_shape=jax.ShapeDtypeStruct((SOURCES, 8, 128), jnp.float32),
        in_specs=[
            pl.BlockSpec(memory_space=pltpu.SMEM),
            pl.BlockSpec(memory_space=VMEM),
            pl.BlockSpec(memory_space=VMEM),
        ],
        out_specs=pl.BlockSpec(memory_space=VMEM),
        name="pack",
    )(assign, kernels.reshape(2, SPAN, SPAN), source_weight.reshape(1, SOURCES))


def window_kernel(ids_ref, mask_a, mask_b, target_a, target_b, own_ref, up_ref, down_ref):
    kern = ids_ref[1]
    odd = lax.rem(kern, 2) == 1

    def cut(left, right, even_start, odd_start):
        left = jnp.where(kern > 0, left, 0.0)
        right = jnp.where(kern < SOURCES - 1, right, 0.0)
        both = jnp.concatenate([left, right], axis=1)
        even = pltpu.roll(both, 256 - even_start, 1)[:, :128]
        other = pltpu.roll(both, 256 - odd_start, 1)[:, :128]
        return jnp.where(odd, other, even).astype(jnp.bfloat16)

    mask = cut(mask_a[...], mask_b[...], 108, 44)
    target = cut(target_a[...].astype(jnp.float32), target_b[...].astype(jnp.float32), 118, 54)
    own_ref[0:64, :] = mask
    own_ref[64:128, :] = target
    up_ref[0:32, :] = mask[0:32]
    up_ref[32:48, :] = target[0:16]
    down_ref[0:32, :] = mask[32:64]
    down_ref[32:48, :] = target[48:64]


def window(ids, mask, target):
    last = mask.shape[1] // 128 - 1

    def left(step, ids):
        return (0, jnp.maximum(lax.div(ids[1] + 1, 2) - 1, 0))

    def right(step, ids):
        return (0, jnp.minimum(lax.div(ids[1] + 1, 2), last))

    return pl.pallas_call(
        window_kernel,
        grid_spec=pltpu.PrefetchScalarGridSpec(
            num_scalar_prefetch=1,
            grid=(1,),
            in_specs=[
                pl.BlockSpec((OWN, 128), left),
                pl.BlockSpec((OWN, 128), right),
                pl.BlockSpec((OWN, 128), left),
                pl.BlockSpec((OWN, 128), right),
            ],
            out_specs=[
                pl.BlockSpec((128, 128), lambda step, ids: (0, 0)),
                pl.BlockSpec((48, 128), lambda step, ids: (0, 0)),
                pl.BlockSpec((48, 128), lambda step, ids: (0, 0)),
            ],
        ),
        out_shape=[
            jax.ShapeDtypeStruct((128, 128), jnp.bfloat16),
            jax.ShapeDtypeStruct((48, 128), jnp.bfloat16),
            jax.ShapeDtypeStruct((48, 128), jnp.bfloat16),
        ],
        name="window",
    )(ids, mask, mask, target, target)


def columns_kernel(ids_ref, own_ref, before_ref, after_ref, cols_ref, aux_ref, side, rows):
    f32 = jnp.float32
    side[0:48, :] = before_ref[...].astype(f32)
    side[48:96, :] = after_ref[...].astype(f32)
    rows[0:20, :] = side[12:32, :]
    rows[20:84, :] = own_ref[0:64, :].astype(f32)
    rows[84:104, :] = side[48:68, :]
    rows[104:112, :] = jnp.zeros((8, 128), f32)
    aux_ref[0, 0:10, :] = side[38:48, :]
    aux_ref[0, 10:74, :] = own_ref[64:128, :].astype(f32)
    aux_ref[0, 74:84, :] = side[80:90, :]
    aux_ref[0, 84:88, :] = jnp.zeros((4, 128), f32)
    row = lax.broadcasted_iota(jnp.int32, (88, 128), 0) + (OWN * ids_ref[0] - HALF)
    col = lax.broadcasted_iota(jnp.int32, (88, 128), 1) + (OWN * ids_ref[1] - HALF)
    inside = (row >= 0) & (row < ids_ref[2]) & (col >= 0) & (col < ids_ref[3])
    aux_ref[1, :, :] = jnp.where(inside, 2.0 * SLOPE, 0.0)
    base = [rows[0:104, :], rows[4:108, :]]
    for first in range(0, SPAN, 2):
        turned = []
        for tap in (first, first + 1):
            if tap >= SPAN:
                turned.append(None)
            else:
                turned.append([pltpu.roll(b, 128 - tap, 1) if tap else b for b in base])
        for group in range(2 * CHUNKS):
            at = 8 * (group // 2)
            one = turned[0][group % 2][at : at + 24]
            if turned[1] is None:
                two = jnp.zeros((8, 128), f32)
            else:
                two = turned[1][group % 2][at : at + 24]
            block = jnp.concatenate([one, two], axis=0).astype(jnp.bfloat16)
            cols_ref[DEPTH * first : DEPTH * first + block.shape[0], 128 * group : 128 * group + 128] = block


def columns(ids, own, before, after):
    return pl.pallas_call(
        columns_kernel,
        out_shape=[
            jax.ShapeDtypeStruct((TAPS, 256 * CHUNKS), jnp.bfloat16),
            jax.ShapeDtypeStruct((2, 88, 128), jnp.float32),
        ],
        in_specs=[pl.BlockSpec(memory_space=pltpu.SMEM)] + [pl.BlockSpec(memory_space=VMEM)] * 3,
        out_specs=[pl.BlockSpec(memory_space=VMEM)] * 2,
        scratch_shapes=[VMEM((96, 128), jnp.float32), VMEM((112, 128), jnp.float32)],
        name="columns",
    )(ids, own, before, after)


def image_kernel(weight_ref, taps_ref, cols_ref, aux_ref, grad_ref, resist_ref, matrix, sums, seen, final):
    f32 = jnp.float32
    base = jnp.concatenate([taps_ref[pl.ds(q, CHANNELS, stride=4), :] for q in range(4)], axis=1)
    weight = base[:, WEIGHT_SLOT : WEIGHT_SLOT + 1]
    for p in range(4):
        moved = pltpu.roll(base, p, 1) if p else base
        matrix[CHANNELS * p : CHANNELS * (p + 1), :] = moved.astype(jnp.bfloat16)
    total = jnp.sum(weight_ref[...], axis=1, keepdims=True)
    inverse = 1.0 / total
    factor = 2.0 * weight * inverse
    for n in range(CHUNKS):
        fields = jnp.dot(matrix[...], cols_ref[:, 256 * n : 256 * n + 256], preferred_element_type=f32)
        parts = []
        for p in range(4):
            field = fields[CHANNELS * p : CHANNELS * (p + 1)]
            aerial = jnp.sum(weight * (field * field), axis=0, keepdims=True) * inverse
            resist = jax.nn.sigmoid(SLOPE * (aerial - LEVEL))
            low, high = 8 * n + p, 8 * n + 4 + p
            target = jnp.concatenate([aux_ref[0, low : low + 1, :], aux_ref[0, high : high + 1, :]], axis=1)
            scale = jnp.concatenate([aux_ref[1, low : low + 1, :], aux_ref[1, high : high + 1, :]], axis=1)
            sense = scale * (resist - target) * resist * (1.0 - resist)
            seen[low : low + 1, :] = resist[:, :128]
            seen[high : high + 1, :] = resist[:, 128:]
            parts.append(((factor * sense) * field).astype(jnp.bfloat16))
        adjoint = jnp.concatenate(parts, axis=0)
        spread = lax.dot_general(matrix[...], adjoint, (((0,), (0,)), ((), ())), preferred_element_type=f32)
        for tap in range(SPAN):
            for third in range(3):
                tile = n + third
                for parity in range(2):
                    if not 2 <= tile <= 10 - parity:
                        continue
                    at = DEPTH * tap + 8 * third
                    piece = spread[at : at + 8, 128 * parity : 128 * parity + 128]
                    spot = 8 * (tile - 2)
                    if third == 2:
                        sums[parity, tap, spot : spot + 8, :] = piece
                    else:
                        sums[parity, tap, spot : spot + 8, :] += piece
    even = sums[0, 0, :, :]
    odd = sums[1, 0, 0:64, :]
    for tap in range(1, SPAN):
        even = even + pltpu.roll(sums[0, tap, :, :], tap, 1)
        odd = odd + pltpu.roll(sums[1, tap, 0:64, :], tap, 1)
    final[...] = even
    grad = final[4:68, :] + odd
    grad_ref[...] = pltpu.roll(grad, 108, 1)[:, :OWN]
    resist_ref[...] = pltpu.roll(seen[10:74, :], 118, 1)[:, :OWN]


def image(source_weight, taps, cols, aux):
    flops = 2 * 2 * 4 * CHANNELS * TAPS * 256 * CHUNKS
    return pl.pallas_call(
        image_kernel,
        out_shape=[
            jax.ShapeDtypeStruct((OWN, OWN), jnp.float32),
            jax.ShapeDtypeStruct((OWN, OWN), jnp.float32),
        ],
        in_specs=[pl.BlockSpec(memory_space=VMEM)] * 4,
        out_specs=[pl.BlockSpec(memory_space=VMEM)] * 2,
        scratch_shapes=[
            VMEM((4 * CHANNELS, TAPS), jnp.bfloat16),
            VMEM((2, SPAN, 72, 128), jnp.float32),
            VMEM((88, 128), jnp.float32),
            VMEM((72, 128), jnp.float32),
        ],
        cost_estimate=pl.CostEstimate(flops=flops, bytes_accessed=4 << 20, transcendentals=0),
        name="image",
    )(source_weight.reshape(1, SOURCES), taps, cols, aux)


def on_device(mask, target, kernels, source_weight, assign):
    tiles = lax.axis_size("tile")
    tile, kern = lax.axis_index("tile"), lax.axis_index("kern")
    ids = jnp.stack([tile, kern, tiles * mask.shape[0], mask.shape[1]]).astype(jnp.int32)
    taps = lax.all_to_all(pack(assign, kernels, source_weight), "kern", split_axis=0, concat_axis=0, tiled=True)
    own, up, down = window(ids, mask, target)
    before = lax.ppermute(down, "tile", [(i, i + 1) for i in range(tiles - 1)])
    after = lax.ppermute(up, "tile", [(i + 1, i) for i in range(tiles - 1)])
    cols, aux = columns(ids, own, before, after)
    grad, resist = image(source_weight, taps.reshape(SOURCES * 8, 128), cols, aux)
    return (grad, resist)


def solution(mesh):
    placed = (P("tile", None), P("tile", None), P("kern", None, None, None), P(), P("kern"))
    return jax.shard_map(
        on_device,
        mesh=mesh,
        in_specs=placed,
        out_specs=(P("tile", "kern"), P("tile", "kern")),
        check_vma=False,
    )
```

```python
import jax
import jax.numpy as jnp
from jax import lax
from jax.experimental import pallas as pl
from jax.experimental.pallas import tpu as pltpu
from jax.sharding import PartitionSpec as P

OWN = 64
SPAN = 21
HALF = 10
SOURCES = 32
CHANNELS = 2 * SOURCES
TILES = 16
DEPTH = 24
TAPS = 512
WEIGHT_SLOT = SPAN * DEPTH
TOTAL_SLOT = WEIGHT_SLOT + 1
CHUNKS = 11
SLOPE = 4.0
LEVEL = 0.6
VMEM = pltpu.VMEM


def in_hbm(array):
    return pltpu.with_memory_space_constraint(array, pltpu.HBM)


def prepare_kernel(
    kern_ref, assign_ref, taps_ref, weight_ref, mask_a, mask_b, target_a, target_b, pack_ref, own_ref, up_ref, down_ref, flat_ref
):
    kern = kern_ref[0]
    odd = lax.rem(kern, 2) == 1
    flat_ref[...] = jnp.zeros_like(flat_ref)
    for i in range(SPAN):
        flat_ref[2 * i : 2 * i + 2, 0:SPAN] = taps_ref[i].astype(jnp.float32)
    slot = lax.broadcasted_iota(jnp.int32, (128, TAPS), 1)
    low = DEPTH * lax.broadcasted_iota(jnp.int32, (128, TAPS), 0)
    spread = ((slot >= low) & (slot < low + DEPTH)).astype(jnp.float32).astype(jnp.bfloat16)
    wide = jnp.dot(flat_ref[...].astype(jnp.bfloat16), spread, preferred_element_type=jnp.float32)
    place = lax.broadcasted_iota(jnp.int32, wide.shape, 1).astype(jnp.float32)
    inner = place - DEPTH * jnp.floor((place + 0.5) * (1.0 / DEPTH))
    twice = 2.0 * inner
    row = lax.broadcasted_iota(jnp.int32, wide.shape, 0).astype(jnp.float32)
    index = lax.broadcasted_iota(jnp.int32, (1, SOURCES), 1)
    weight = jnp.sum(jnp.where(index == assign_ref[...], weight_ref[...], 0.0), axis=1, keepdims=True)
    total = jnp.sum(weight_ref[...], axis=1, keepdims=True)
    lane = lax.broadcasted_iota(jnp.int32, (1, TAPS), 1)
    rows = []
    for part in range(2):
        flat = jnp.sum(jnp.where(row == twice + part, wide, 0.0), axis=0, keepdims=True)
        flat = jnp.where(lane == WEIGHT_SLOT, weight, jnp.where(lane == TOTAL_SLOT, total, flat))
        rows += [flat[:, 128 * q : 128 * q + 128] for q in range(4)]
    pack_ref[...] = jnp.broadcast_to(jnp.concatenate(rows, axis=0)[None], pack_ref.shape)

    def cut(left, right, even_start, odd_start):
        left = jnp.where(kern > 0, left, 0.0)
        right = jnp.where(kern < SOURCES - 1, right, 0.0)
        both = jnp.concatenate([left, right], axis=1)
        even = pltpu.roll(both, 256 - even_start, 1)[:, :128]
        other = pltpu.roll(both, 256 - odd_start, 1)[:, :128]
        return jnp.where(odd, other, even).astype(jnp.bfloat16)

    mask = cut(mask_a[...], mask_b[...], 108, 44)
    target = cut(target_a[...].astype(jnp.float32), target_b[...].astype(jnp.float32), 118, 54)
    own_ref[0:64, :] = mask
    own_ref[64:128, :] = target
    up_ref[0:32, :] = mask[0:32]
    up_ref[32:48, :] = target[0:16]
    down_ref[0:32, :] = mask[32:64]
    down_ref[32:48, :] = target[48:64]


def prepare(kern, assign, kernels, source_weight, mask, target):
    last = mask.shape[1] // 128 - 1

    def left(step, kern):
        return (0, jnp.maximum(lax.div(kern[0] + 1, 2) - 1, 0))

    def right(step, kern):
        return (0, jnp.minimum(lax.div(kern[0] + 1, 2), last))

    def zeros(rank):
        return lambda step, kern: (0,) * rank

    mask, target = in_hbm(mask), in_hbm(target)
    return pl.pallas_call(
        prepare_kernel,
        grid_spec=pltpu.PrefetchScalarGridSpec(
            num_scalar_prefetch=1,
            grid=(1,),
            in_specs=[
                pl.BlockSpec((1, 1), zeros(2)),
                pl.BlockSpec((SPAN, 2, SPAN), zeros(3)),
                pl.BlockSpec((1, SOURCES), zeros(2)),
                pl.BlockSpec((OWN, 128), left),
                pl.BlockSpec((OWN, 128), right),
                pl.BlockSpec((OWN, 128), left),
                pl.BlockSpec((OWN, 128), right),
            ],
            out_specs=[
                pl.BlockSpec((SOURCES, 8, 128), zeros(3)),
                pl.BlockSpec((128, 128), zeros(2)),
                pl.BlockSpec((48, 128), zeros(2)),
                pl.BlockSpec((48, 128), zeros(2)),
            ],
            scratch_shapes=[VMEM((48, 128), jnp.float32)],
        ),
        out_shape=[
            jax.ShapeDtypeStruct((SOURCES, 8, 128), jnp.float32),
            jax.ShapeDtypeStruct((128, 128), jnp.bfloat16),
            jax.ShapeDtypeStruct((48, 128), jnp.bfloat16),
            jax.ShapeDtypeStruct((48, 128), jnp.bfloat16),
        ],
        compiler_params=pltpu.CompilerParams(vmem_limit_bytes=8 << 20),
        name="prepare",
    )(
        kern,
        assign.reshape(1, 1),
        in_hbm(kernels.transpose(0, 2, 1, 3).reshape(SPAN, 2, SPAN)),
        in_hbm(source_weight.reshape(1, SOURCES)),
        mask,
        mask,
        target,
        target,
    )


def columns_kernel(tile_ref, kern_ref, own_ref, before_ref, after_ref, cols_ref, aux_ref, side, rows):
    f32 = jnp.float32
    side[0:48, :] = before_ref[...].astype(f32)
    side[48:96, :] = after_ref[...].astype(f32)
    rows[0:20, :] = side[12:32, :]
    rows[20:84, :] = own_ref[0:64, :].astype(f32)
    rows[84:104, :] = side[48:68, :]
    rows[104:112, :] = jnp.zeros((8, 128), f32)
    aux_ref[0, 0:10, :] = side[38:48, :]
    aux_ref[0, 10:74, :] = own_ref[64:128, :].astype(f32)
    aux_ref[0, 74:84, :] = side[80:90, :]
    aux_ref[0, 84:88, :] = jnp.zeros((4, 128), f32)
    row = lax.broadcasted_iota(jnp.int32, (88, 128), 0) + (OWN * tile_ref[0] - HALF)
    col = lax.broadcasted_iota(jnp.int32, (88, 128), 1) + (OWN * kern_ref[0] - HALF)
    inside = (row >= 0) & (row < OWN * TILES) & (col >= 0) & (col < OWN * SOURCES)
    aux_ref[1, :, :] = jnp.where(inside, 2.0 * SLOPE, 0.0)
    base = [rows[0:104, :], rows[4:108, :]]
    for first in range(0, SPAN, 2):
        turned = []
        for tap in (first, first + 1):
            if tap >= SPAN:
                turned.append(None)
            else:
                turned.append([pltpu.roll(b, 128 - tap, 1) if tap else b for b in base])
        for group in range(2 * CHUNKS):
            at = 8 * (group // 2)
            one = turned[0][group % 2][at : at + 24]
            if turned[1] is None:
                two = jnp.zeros((8, 128), f32)
            else:
                two = turned[1][group % 2][at : at + 24]
            block = jnp.concatenate([one, two], axis=0).astype(jnp.bfloat16)
            cols_ref[DEPTH * first : DEPTH * first + block.shape[0], 128 * group : 128 * group + 128] = block


def columns(tile, kern, own, before, after):
    return pl.pallas_call(
        columns_kernel,
        out_shape=[
            jax.ShapeDtypeStruct((TAPS, 256 * CHUNKS), jnp.bfloat16),
            jax.ShapeDtypeStruct((2, 88, 128), jnp.float32),
        ],
        in_specs=[pl.BlockSpec(memory_space=pltpu.SMEM)] * 2 + [pl.BlockSpec(memory_space=VMEM)] * 3,
        out_specs=[pl.BlockSpec(memory_space=VMEM)] * 2,
        scratch_shapes=[VMEM((96, 128), jnp.float32), VMEM((112, 128), jnp.float32)],
        compiler_params=pltpu.CompilerParams(vmem_limit_bytes=12 << 20),
        cost_estimate=pl.CostEstimate(flops=1 << 20, bytes_accessed=4 << 20, transcendentals=0),
        name="columns",
    )(tile, kern, own, before, after)


def image_kernel(taps_ref, cols_ref, aux_ref, grad_ref, resist_ref, matrix, sums, seen, final):
    f32 = jnp.float32
    base = jnp.concatenate([taps_ref[pl.ds(q, CHANNELS, stride=4), :] for q in range(4)], axis=1)
    weight = base[:, WEIGHT_SLOT : WEIGHT_SLOT + 1]
    for p in range(4):
        moved = pltpu.roll(base, p, 1) if p else base
        matrix[CHANNELS * p : CHANNELS * (p + 1), :] = moved.astype(jnp.bfloat16)
    inverse = 1.0 / base[0:1, TOTAL_SLOT : TOTAL_SLOT + 1]
    factor = 2.0 * weight * inverse
    for n in range(CHUNKS):
        fields = jnp.dot(matrix[...], cols_ref[:, 256 * n : 256 * n + 256], preferred_element_type=f32)
        parts = []
        for p in range(4):
            field = fields[CHANNELS * p : CHANNELS * (p + 1)]
            aerial = jnp.sum(weight * (field * field), axis=0, keepdims=True) * inverse
            resist = jax.nn.sigmoid(SLOPE * (aerial - LEVEL))
            low, high = 8 * n + p, 8 * n + 4 + p
            target = jnp.concatenate([aux_ref[0, low : low + 1, :], aux_ref[0, high : high + 1, :]], axis=1)
            scale = jnp.concatenate([aux_ref[1, low : low + 1, :], aux_ref[1, high : high + 1, :]], axis=1)
            sense = scale * (resist - target) * resist * (1.0 - resist)
            seen[low : low + 1, :] = resist[:, :128]
            seen[high : high + 1, :] = resist[:, 128:]
            parts.append(((factor * sense) * field).astype(jnp.bfloat16))
        adjoint = jnp.concatenate(parts, axis=0)
        spread = lax.dot_general(matrix[...], adjoint, (((0,), (0,)), ((), ())), preferred_element_type=f32)
        for tap in range(SPAN):
            for third in range(3):
                tile = n + third
                for parity in range(2):
                    if not 2 <= tile <= 10 - parity:
                        continue
                    at = DEPTH * tap + 8 * third
                    piece = spread[at : at + 8, 128 * parity : 128 * parity + 128]
                    spot = 8 * (tile - 2)
                    if third == 2:
                        sums[parity, tap, spot : spot + 8, :] = piece
                    else:
                        sums[parity, tap, spot : spot + 8, :] += piece
    even = sums[0, 0, :, :]
    odd = sums[1, 0, 0:64, :]
    for tap in range(1, SPAN):
        even = even + pltpu.roll(sums[0, tap, :, :], tap, 1)
        odd = odd + pltpu.roll(sums[1, tap, 0:64, :], tap, 1)
    final[...] = even
    grad = final[4:68, :] + odd
    grad_ref[...] = pltpu.roll(grad, 108, 1)[:, :OWN]
    resist_ref[...] = pltpu.roll(seen[10:74, :], 118, 1)[:, :OWN]


def image(taps, cols, aux):
    flops = 2 * 2 * 4 * CHANNELS * TAPS * 256 * CHUNKS
    return pl.pallas_call(
        image_kernel,
        out_shape=[
            jax.ShapeDtypeStruct((OWN, OWN), jnp.float32),
            jax.ShapeDtypeStruct((OWN, OWN), jnp.float32),
        ],
        in_specs=[pl.BlockSpec(memory_space=VMEM)] * 3,
        out_specs=[pl.BlockSpec(memory_space=VMEM)] * 2,
        scratch_shapes=[
            VMEM((4 * CHANNELS, TAPS), jnp.bfloat16),
            VMEM((2, SPAN, 72, 128), jnp.float32),
            VMEM((88, 128), jnp.float32),
            VMEM((72, 128), jnp.float32),
        ],
        cost_estimate=pl.CostEstimate(flops=flops, bytes_accessed=4 << 20, transcendentals=0),
        compiler_params=pltpu.CompilerParams(vmem_limit_bytes=20 << 20),
        name="image",
    )(taps, cols, aux)


def on_device(mask, target, kernels, source_weight, assign):
    tiles = lax.axis_size("tile")
    tile = lax.axis_index("tile").astype(jnp.int32).reshape(1)
    kern = lax.axis_index("kern").astype(jnp.int32).reshape(1)
    sent, own, up, down = prepare(kern, assign, kernels, source_weight, mask, target)
    taps = lax.all_to_all(sent, "kern", split_axis=0, concat_axis=0, tiled=True)
    before = lax.ppermute(down, "tile", [(i, i + 1) for i in range(tiles - 1)])
    after = lax.ppermute(up, "tile", [(i + 1, i) for i in range(tiles - 1)])
    cols, aux = columns(tile, kern, own, before, after)
    grad, resist = image(taps.reshape(SOURCES * 8, 128), cols, aux)
    return (grad, resist)


def solution(mesh):
    placed = (P("tile", None), P("tile", None), P("kern", None, None, None), P(), P("kern"))
    return jax.shard_map(
        on_device,
        mesh=mesh,
        in_specs=placed,
        out_specs=(P("tile", "kern"), P("tile", "kern")),
        check_vma=False,
    )
```

```python
import jax
import jax.numpy as jnp
from jax import lax
from jax.experimental import pallas as pl
from jax.experimental.pallas import tpu as pltpu
from jax.sharding import PartitionSpec as P

OWN = 64
SPAN = 21
HALF = 10
SOURCES = 32
CHANNELS = 2 * SOURCES
TILES = 16
DEPTH = 24
TAPS = 512
WEIGHT_SLOT = SPAN * DEPTH
CHUNKS = 11
BAND = 8 * SPAN + 8
SLOPE = 4.0
LEVEL = 0.6
VMEM = pltpu.VMEM


def in_hbm(array):
    return pltpu.with_memory_space_constraint(array, pltpu.HBM)


def pack_kernel(assign_ref, taps_ref, weight_ref, pack_ref, flat_ref):
    flat_ref[...] = jnp.zeros_like(flat_ref)
    for i in range(SPAN):
        flat_ref[2 * i : 2 * i + 2, 0:SPAN] = taps_ref[i].astype(jnp.float32)
    slot = lax.broadcasted_iota(jnp.int32, (128, TAPS), 1)
    low = DEPTH * lax.broadcasted_iota(jnp.int32, (128, TAPS), 0)
    spread = ((slot >= low) & (slot < low + DEPTH)).astype(jnp.float32).astype(jnp.bfloat16)
    wide = jnp.dot(flat_ref[...].astype(jnp.bfloat16), spread, preferred_element_type=jnp.float32)
    place = lax.broadcasted_iota(jnp.int32, wide.shape, 1).astype(jnp.float32)
    inner = place - DEPTH * jnp.floor((place + 0.5) * (1.0 / DEPTH))
    twice = 2.0 * inner
    row = lax.broadcasted_iota(jnp.int32, wide.shape, 0).astype(jnp.float32)
    index = lax.broadcasted_iota(jnp.int32, (1, SOURCES), 1)
    weight = jnp.sum(jnp.where(index == assign_ref[...], weight_ref[...], 0.0), axis=1, keepdims=True)
    lane = lax.broadcasted_iota(jnp.int32, (1, TAPS), 1)
    first = weight.astype(jnp.bfloat16).astype(jnp.float32)
    second = (weight - first).astype(jnp.bfloat16).astype(jnp.float32)
    third = weight - first - second
    rows = []
    for part in range(2):
        flat = jnp.sum(jnp.where(row == twice + part, wide, 0.0), axis=0, keepdims=True)
        for place, value in enumerate((first, second, third)):
            flat = jnp.where(lane == WEIGHT_SLOT + place, value, flat)
        rows += [flat[:, 128 * q : 128 * q + 128] for q in range(4)]
    pack_ref[...] = jnp.broadcast_to(jnp.concatenate(rows, axis=0).astype(jnp.bfloat16)[None], pack_ref.shape)


def pack(assign, kernels, source_weight):
    return pl.pallas_call(
        pack_kernel,
        out_shape=jax.ShapeDtypeStruct((SOURCES, 8, 128), jnp.bfloat16),
        in_specs=[pl.BlockSpec(memory_space=VMEM)] * 3,
        out_specs=pl.BlockSpec(memory_space=VMEM),
        scratch_shapes=[VMEM((48, 128), jnp.float32)],
        compiler_params=pltpu.CompilerParams(vmem_limit_bytes=8 << 20),
        name="pack",
    )(
        assign.reshape(1, 1),
        in_hbm(kernels.transpose(0, 2, 1, 3).reshape(SPAN, 2, SPAN)),
        in_hbm(source_weight.reshape(1, SOURCES)),
    )


def window_kernel(tile_ref, kern_ref, mask_a, mask_b, target_a, target_b, own_ref, near_ref, far_ref):
    kern = kern_ref[0]
    odd = lax.rem(kern, 2) == 1

    def cut(left, right, even_start, odd_start):
        left = jnp.where(kern > 0, left, 0.0)
        right = jnp.where(kern < SOURCES - 1, right, 0.0)
        both = jnp.concatenate([left, right], axis=1)
        even = pltpu.roll(both, 256 - even_start, 1)[:, :128]
        other = pltpu.roll(both, 256 - odd_start, 1)[:, :128]
        return jnp.where(odd, other, even).astype(jnp.bfloat16)

    mask = cut(mask_a[...], mask_b[...], 108, 44)
    target = cut(target_a[...].astype(jnp.float32), target_b[...].astype(jnp.float32), 118, 54)
    own_ref[0:64, :] = mask
    own_ref[64:128, :] = target
    even = lax.rem(tile_ref[0], 2) == 0
    near_ref[0:32, :] = jnp.where(even, mask[32:64], mask[0:32])
    near_ref[32:48, :] = jnp.where(even, target[48:64], target[0:16])
    far_ref[0:32, :] = jnp.where(even, mask[0:32], mask[32:64])
    far_ref[32:48, :] = jnp.where(even, target[0:16], target[48:64])


def window(tile, kern, mask, target):
    last = mask.shape[1] // 128 - 1

    def left(step, tile, kern):
        return (0, jnp.maximum(lax.div(kern[0] + 1, 2) - 1, 0))

    def right(step, tile, kern):
        return (0, jnp.minimum(lax.div(kern[0] + 1, 2), last))

    def zeros(rank):
        return lambda step, tile, kern: (0,) * rank

    mask, target = in_hbm(mask), in_hbm(target)
    return pl.pallas_call(
        window_kernel,
        grid_spec=pltpu.PrefetchScalarGridSpec(
            num_scalar_prefetch=2,
            grid=(1,),
            in_specs=[
                pl.BlockSpec((OWN, 128), left),
                pl.BlockSpec((OWN, 128), right),
                pl.BlockSpec((OWN, 128), left),
                pl.BlockSpec((OWN, 128), right),
            ],
            out_specs=[
                pl.BlockSpec((128, 128), zeros(2)),
                pl.BlockSpec((48, 128), zeros(2)),
                pl.BlockSpec((48, 128), zeros(2)),
            ],
        ),
        out_shape=[
            jax.ShapeDtypeStruct((128, 128), jnp.bfloat16),
            jax.ShapeDtypeStruct((48, 128), jnp.bfloat16),
            jax.ShapeDtypeStruct((48, 128), jnp.bfloat16),
        ],
        compiler_params=pltpu.CompilerParams(vmem_limit_bytes=8 << 20),
        name="window",
    )(
        tile,
        kern,
        mask,
        mask,
        target,
        target,
    )


def columns_kernel(tile_ref, kern_ref, own_ref, near_ref, far_ref, cols_ref, aux_ref, side, rows):
    f32 = jnp.float32
    even = lax.rem(tile_ref[0], 2) == 0
    near, far = near_ref[...].astype(f32), far_ref[...].astype(f32)
    side[0:48, :] = jnp.where(even, far, near)
    side[48:96, :] = jnp.where(even, near, far)
    rows[0:20, :] = side[12:32, :]
    rows[20:84, :] = own_ref[0:64, :].astype(f32)
    rows[84:104, :] = side[48:68, :]
    rows[104:112, :] = jnp.zeros((8, 128), f32)
    aux_ref[0, 0:10, :] = side[38:48, :]
    aux_ref[0, 10:74, :] = own_ref[64:128, :].astype(f32)
    aux_ref[0, 74:84, :] = side[80:90, :]
    aux_ref[0, 84:88, :] = jnp.zeros((4, 128), f32)
    row = lax.broadcasted_iota(jnp.int32, (88, 128), 0) + (OWN * tile_ref[0] - HALF)
    col = lax.broadcasted_iota(jnp.int32, (88, 128), 1) + (OWN * kern_ref[0] - HALF)
    inside = (row >= 0) & (row < OWN * TILES) & (col >= 0) & (col < OWN * SOURCES)
    aux_ref[1, :, :] = jnp.where(inside, 2.0 * SLOPE, 0.0)
    base = [rows[0:104, :], rows[4:108, :]]
    for first in range(0, SPAN, 2):
        turned = []
        for tap in (first, first + 1):
            if tap >= SPAN:
                turned.append(None)
            else:
                turned.append([pltpu.roll(b, 128 - tap, 1) if tap else b for b in base])
        for group in range(2 * CHUNKS):
            at = 8 * (group // 2)
            one = turned[0][group % 2][at : at + 24]
            if turned[1] is None:
                two = jnp.zeros((8, 128), f32)
            else:
                two = turned[1][group % 2][at : at + 24]
            block = jnp.concatenate([one, two], axis=0).astype(jnp.bfloat16)
            cols_ref[DEPTH * first : DEPTH * first + block.shape[0], 128 * group : 128 * group + 128] = block


def columns(tile, kern, own, near, far):
    return pl.pallas_call(
        columns_kernel,
        out_shape=[
            jax.ShapeDtypeStruct((TAPS, 256 * CHUNKS), jnp.bfloat16),
            jax.ShapeDtypeStruct((2, 88, 128), jnp.float32),
        ],
        in_specs=[pl.BlockSpec(memory_space=pltpu.SMEM)] * 2 + [pl.BlockSpec(memory_space=VMEM)] * 3,
        out_specs=[pl.BlockSpec(memory_space=VMEM)] * 2,
        scratch_shapes=[VMEM((96, 128), jnp.float32), VMEM((112, 128), jnp.float32)],
        compiler_params=pltpu.CompilerParams(vmem_limit_bytes=12 << 20),
        cost_estimate=pl.CostEstimate(flops=1 << 20, bytes_accessed=4 << 20, transcendentals=0),
        name="columns",
    )(tile, kern, own, near, far)


def image_kernel(taps_ref, cols_ref, aux_ref, grad_ref, resist_ref, wide, matrix, turned, fields, adjoint, sums, seen, final):
    f32 = jnp.float32
    wide[...] = taps_ref[...].astype(f32)
    base = jnp.concatenate([wide[pl.ds(q, CHANNELS, stride=4), :] for q in range(4)], axis=1)
    weight = base[:, WEIGHT_SLOT : WEIGHT_SLOT + 1] + base[:, WEIGHT_SLOT + 1 : WEIGHT_SLOT + 2]
    weight = weight + base[:, WEIGHT_SLOT + 2 : WEIGHT_SLOT + 3]
    moved = jnp.concatenate([pltpu.roll(base, p, 1) if p else base for p in range(4)], axis=0)
    matrix[...] = moved.astype(jnp.bfloat16)
    upright = jnp.transpose(moved)
    for third in range(3):
        starts = [DEPTH * tap + 8 * third for tap in range(SPAN)]
        rows = [upright[at : at + 8] for at in starts] + [jnp.zeros((8, 4 * CHANNELS), f32)]
        turned[BAND * third : BAND * (third + 1), :] = jnp.concatenate(rows, axis=0).astype(jnp.bfloat16)
    inverse = 2.0 / jnp.sum(weight, axis=0, keepdims=True)
    twice = 2.0 * inverse
    def groups_of(n):
        return [2 * n, 2 * n + 1] if n < CHUNKS - 1 else [2 * n]

    def image_of(n):
        width = 128 * len(groups_of(n))
        cols = cols_ref[:, 256 * n : 256 * n + width]
        fields[n % 2, :, 0:width] = jnp.dot(matrix[...], cols, preferred_element_type=f32)

    def adjoint_of(n):
        groups = groups_of(n)
        width = 128 * len(groups)
        for p in range(4):
            field = fields[n % 2, CHANNELS * p : CHANNELS * (p + 1), 0:width]
            heavy = weight * field
            aerial = jnp.sum(heavy * field, axis=0, keepdims=True) * inverse
            resist = jax.nn.sigmoid(SLOPE * (aerial - LEVEL))
            spots = [4 * group + p for group in groups]
            target = jnp.concatenate([aux_ref[0, spot : spot + 1, :] for spot in spots], axis=1)
            scale = jnp.concatenate([aux_ref[1, spot : spot + 1, :] for spot in spots], axis=1)
            sense = scale * (resist - target) * resist * (1.0 - resist)
            for parity, spot in enumerate(spots):
                seen[spot : spot + 1, :] = resist[:, 128 * parity : 128 * parity + 128]
            value = (heavy * (twice * sense)).astype(jnp.bfloat16)
            adjoint[n % 2, CHANNELS * p : CHANNELS * (p + 1), 0:width] = value

    def spread_of(n):
        groups = groups_of(n)
        low, high = max(0, 2 - n), min(3, 11 - n)
        moved_in = adjoint[n % 2, :, 0 : 128 * len(groups)]
        spread = jnp.dot(turned[BAND * low : BAND * high, :], moved_in, preferred_element_type=f32)
        for third in range(low, high):
            tile = n + third
            for parity in range(len(groups)):
                if tile > 10 - parity:
                    continue
                at = BAND * (third - low)
                piece = spread[at : at + 8 * SPAN, 128 * parity : 128 * parity + 128]
                if third == 2:
                    sums[parity, tile - 2, :, :] = piece
                else:
                    sums[parity, tile - 2, :, :] += piece

    for step in range(CHUNKS + 2):
        if step < CHUNKS:
            image_of(step)
        if 0 <= step - 2:
            spread_of(step - 2)
        if 0 <= step - 1 < CHUNKS:
            adjoint_of(step - 1)
    totals = []
    for parity in range(2):
        total = None
        for tap in range(SPAN):
            part = jnp.concatenate([sums[parity, at, 8 * tap : 8 * tap + 8, :] for at in range(9 - parity)], axis=0)
            part = pltpu.roll(part, tap, 1) if tap else part
            total = part if total is None else total + part
        totals.append(total)
    final[...] = totals[0]
    grad = final[4:68, :] + totals[1]
    grad_ref[...] = pltpu.roll(grad, 108, 1)[:, :OWN]
    resist_ref[...] = pltpu.roll(seen[10:74, :], 118, 1)[:, :OWN]


def image(taps, cols, aux):
    flops = 2 * 2 * 4 * CHANNELS * TAPS * 256 * CHUNKS
    return pl.pallas_call(
        image_kernel,
        out_shape=[
            jax.ShapeDtypeStruct((OWN, OWN), jnp.float32),
            jax.ShapeDtypeStruct((OWN, OWN), jnp.float32),
        ],
        in_specs=[pl.BlockSpec(memory_space=VMEM)] * 3,
        out_specs=[pl.BlockSpec(memory_space=VMEM)] * 2,
        scratch_shapes=[
            VMEM((8 * SOURCES, 128), jnp.float32),
            VMEM((4 * CHANNELS, TAPS), jnp.bfloat16),
            VMEM((3 * BAND, 4 * CHANNELS), jnp.bfloat16),
            VMEM((2, 4 * CHANNELS, 256), jnp.float32),
            VMEM((2, 4 * CHANNELS, 256), jnp.bfloat16),
            VMEM((2, 9, 8 * SPAN, 128), jnp.float32),
            VMEM((88, 128), jnp.float32),
            VMEM((72, 128), jnp.float32),
        ],
        cost_estimate=pl.CostEstimate(flops=flops, bytes_accessed=4 << 20, transcendentals=0),
        compiler_params=pltpu.CompilerParams(vmem_limit_bytes=20 << 20),
        name="image",
    )(taps, cols, aux)


def on_device(mask, target, kernels, source_weight, assign):
    tiles = lax.axis_size("tile")
    tile = lax.axis_index("tile").astype(jnp.int32).reshape(1)
    kern = lax.axis_index("kern").astype(jnp.int32).reshape(1)
    sent = pack(assign, kernels, source_weight)
    own, near, far = window(tile, kern, mask, target)
    taps = lax.all_to_all(sent, "kern", split_axis=0, concat_axis=0, tiled=True)

    def swapped(part, first):
        pairs = [(i, i + 1) for i in range(first, tiles - 1, 2)]
        return lax.ppermute(part, "tile", pairs + [(j, i) for i, j in pairs])

    far = swapped(far, 1)
    near = swapped(near, 0)
    cols, aux = columns(tile, kern, own, near, far)
    grad, resist = image(taps.reshape(SOURCES * 8, 128), cols, aux)
    return (grad, resist)


def solution(mesh):
    placed = (P("tile", None), P("tile", None), P("kern", None, None, None), P(), P("kern"))
    return jax.shard_map(
        on_device,
        mesh=mesh,
        in_specs=placed,
        out_specs=(P("tile", "kern"), P("tile", "kern")),
        check_vma=False,
    )
```

```python
import jax
import jax.numpy as jnp
from jax import lax
from jax.experimental import pallas as pl
from jax.experimental.pallas import tpu as pltpu
from jax.sharding import PartitionSpec as P

OWN = 64
SPAN = 21
HALF = 10
SOURCES = 32
CHANNELS = 2 * SOURCES
TILES = 16
DEPTH = 24
TAPS = 512
WEIGHT_SLOT = SPAN * DEPTH
CHUNKS = 11
BAND = 8 * SPAN + 8
SLOPE = 4.0
LEVEL = 0.6
VMEM = pltpu.VMEM


def in_hbm(array):
    return pltpu.with_memory_space_constraint(array, pltpu.HBM)


def pack_kernel(assign_ref, taps_ref, weight_ref, pack_ref, flat_ref):
    flat_ref[...] = jnp.zeros_like(flat_ref)
    for i in range(SPAN):
        flat_ref[2 * i : 2 * i + 2, 0:SPAN] = taps_ref[i].astype(jnp.float32)
    slot = lax.broadcasted_iota(jnp.int32, (128, TAPS), 1)
    low = DEPTH * lax.broadcasted_iota(jnp.int32, (128, TAPS), 0)
    spread = ((slot >= low) & (slot < low + DEPTH)).astype(jnp.float32).astype(jnp.bfloat16)
    wide = jnp.dot(flat_ref[...].astype(jnp.bfloat16), spread, preferred_element_type=jnp.float32)
    place = lax.broadcasted_iota(jnp.int32, wide.shape, 1).astype(jnp.float32)
    inner = place - DEPTH * jnp.floor((place + 0.5) * (1.0 / DEPTH))
    twice = 2.0 * inner
    row = lax.broadcasted_iota(jnp.int32, wide.shape, 0).astype(jnp.float32)
    index = lax.broadcasted_iota(jnp.int32, (1, SOURCES), 1)
    weight = jnp.sum(jnp.where(index == assign_ref[...], weight_ref[...], 0.0), axis=1, keepdims=True)
    lane = lax.broadcasted_iota(jnp.int32, (1, TAPS), 1)
    first = weight.astype(jnp.bfloat16).astype(jnp.float32)
    second = (weight - first).astype(jnp.bfloat16).astype(jnp.float32)
    third = weight - first - second
    rows = []
    for part in range(2):
        flat = jnp.sum(jnp.where(row == twice + part, wide, 0.0), axis=0, keepdims=True)
        for place, value in enumerate((first, second, third)):
            flat = jnp.where(lane == WEIGHT_SLOT + place, value, flat)
        rows += [flat[:, 128 * q : 128 * q + 128] for q in range(4)]
    pack_ref[...] = jnp.broadcast_to(jnp.concatenate(rows, axis=0).astype(jnp.bfloat16)[None], pack_ref.shape)


def pack(assign, kernels, source_weight):
    return pl.pallas_call(
        pack_kernel,
        out_shape=jax.ShapeDtypeStruct((SOURCES, 8, 128), jnp.bfloat16),
        in_specs=[pl.BlockSpec(memory_space=VMEM)] * 3,
        out_specs=pl.BlockSpec(memory_space=VMEM),
        scratch_shapes=[VMEM((48, 128), jnp.float32)],
        compiler_params=pltpu.CompilerParams(vmem_limit_bytes=8 << 20),
        name="pack",
    )(
        assign.reshape(1, 1),
        in_hbm(kernels.transpose(0, 2, 1, 3).reshape(SPAN, 2, SPAN)),
        in_hbm(source_weight.reshape(1, SOURCES)),
    )


def window_kernel(tile_ref, kern_ref, mask_a, mask_b, target_a, target_b, own_ref, near_ref, far_ref):
    kern = kern_ref[0]
    odd = lax.rem(kern, 2) == 1

    def cut(left, right, even_start, odd_start):
        left = jnp.where(kern > 0, left, 0.0)
        right = jnp.where(kern < SOURCES - 1, right, 0.0)
        both = jnp.concatenate([left, right], axis=1)
        even = pltpu.roll(both, 256 - even_start, 1)[:, :128]
        other = pltpu.roll(both, 256 - odd_start, 1)[:, :128]
        return jnp.where(odd, other, even).astype(jnp.bfloat16)

    mask = cut(mask_a[...], mask_b[...], 108, 44)
    target = cut(target_a[...].astype(jnp.float32), target_b[...].astype(jnp.float32), 118, 54)
    own_ref[0:64, :] = mask
    own_ref[64:128, :] = target
    even = lax.rem(tile_ref[0], 2) == 0
    near_ref[0:32, :] = jnp.where(even, mask[32:64], mask[0:32])
    near_ref[32:48, :] = jnp.where(even, target[48:64], target[0:16])
    far_ref[0:32, :] = jnp.where(even, mask[0:32], mask[32:64])
    far_ref[32:48, :] = jnp.where(even, target[0:16], target[48:64])


def window(tile, kern, mask, target):
    last = mask.shape[1] // 128 - 1

    def left(step, tile, kern):
        return (0, jnp.maximum(lax.div(kern[0] + 1, 2) - 1, 0))

    def right(step, tile, kern):
        return (0, jnp.minimum(lax.div(kern[0] + 1, 2), last))

    def zeros(rank):
        return lambda step, tile, kern: (0,) * rank

    mask, target = in_hbm(mask), in_hbm(target)
    return pl.pallas_call(
        window_kernel,
        grid_spec=pltpu.PrefetchScalarGridSpec(
            num_scalar_prefetch=2,
            grid=(1,),
            in_specs=[
                pl.BlockSpec((OWN, 128), left),
                pl.BlockSpec((OWN, 128), right),
                pl.BlockSpec((OWN, 128), left),
                pl.BlockSpec((OWN, 128), right),
            ],
            out_specs=[
                pl.BlockSpec((128, 128), zeros(2)),
                pl.BlockSpec((48, 128), zeros(2)),
                pl.BlockSpec((48, 128), zeros(2)),
            ],
        ),
        out_shape=[
            jax.ShapeDtypeStruct((128, 128), jnp.bfloat16),
            jax.ShapeDtypeStruct((48, 128), jnp.bfloat16),
            jax.ShapeDtypeStruct((48, 128), jnp.bfloat16),
        ],
        compiler_params=pltpu.CompilerParams(vmem_limit_bytes=8 << 20),
        name="window",
    )(
        tile,
        kern,
        mask,
        mask,
        target,
        target,
    )


def columns_kernel(tile_ref, kern_ref, own_ref, near_ref, far_ref, cols_ref, aux_ref, side, rows):
    f32 = jnp.float32
    even = lax.rem(tile_ref[0], 2) == 0
    near, far = near_ref[...].astype(f32), far_ref[...].astype(f32)
    side[0:48, :] = jnp.where(even, far, near)
    side[48:96, :] = jnp.where(even, near, far)
    rows[0:20, :] = side[12:32, :]
    rows[20:84, :] = own_ref[0:64, :].astype(f32)
    rows[84:104, :] = side[48:68, :]
    rows[104:112, :] = jnp.zeros((8, 128), f32)
    aux_ref[0, 0:10, :] = side[38:48, :]
    aux_ref[0, 10:74, :] = own_ref[64:128, :].astype(f32)
    aux_ref[0, 74:84, :] = side[80:90, :]
    aux_ref[0, 84:88, :] = jnp.zeros((4, 128), f32)
    row = lax.broadcasted_iota(jnp.int32, (88, 128), 0) + (OWN * tile_ref[0] - HALF)
    col = lax.broadcasted_iota(jnp.int32, (88, 128), 1) + (OWN * kern_ref[0] - HALF)
    inside = (row >= 0) & (row < OWN * TILES) & (col >= 0) & (col < OWN * SOURCES)
    aux_ref[1, :, :] = jnp.where(inside, 2.0 * SLOPE, 0.0)
    base = [rows[0:104, :], rows[4:108, :]]
    for first in range(0, SPAN, 2):
        turned = []
        for tap in (first, first + 1):
            if tap >= SPAN:
                turned.append(None)
            else:
                turned.append([pltpu.roll(b, 128 - tap, 1) if tap else b for b in base])
        for group in range(2 * CHUNKS):
            at = 8 * (group // 2)
            one = turned[0][group % 2][at : at + 24]
            if turned[1] is None:
                two = jnp.zeros((8, 128), f32)
            else:
                two = turned[1][group % 2][at : at + 24]
            block = jnp.concatenate([one, two], axis=0).astype(jnp.bfloat16)
            cols_ref[DEPTH * first : DEPTH * first + block.shape[0], 128 * group : 128 * group + 128] = block


def columns(tile, kern, own, near, far):
    return pl.pallas_call(
        columns_kernel,
        out_shape=[
            jax.ShapeDtypeStruct((TAPS, 256 * CHUNKS), jnp.bfloat16),
            jax.ShapeDtypeStruct((2, 88, 128), jnp.float32),
        ],
        in_specs=[pl.BlockSpec(memory_space=pltpu.SMEM)] * 2 + [pl.BlockSpec(memory_space=VMEM)] * 3,
        out_specs=[pl.BlockSpec(memory_space=VMEM)] * 2,
        scratch_shapes=[VMEM((96, 128), jnp.float32), VMEM((112, 128), jnp.float32)],
        compiler_params=pltpu.CompilerParams(vmem_limit_bytes=12 << 20),
        cost_estimate=pl.CostEstimate(flops=1 << 20, bytes_accessed=4 << 20, transcendentals=0),
        name="columns",
    )(tile, kern, own, near, far)


def image_kernel(taps_ref, cols_ref, aux_ref, grad_out, resist_out, grad_ref, resist_ref, done, wide, matrix, turned, fields, adjoint, sums, seen, final):
    f32 = jnp.float32
    wide[...] = taps_ref[...].astype(f32)
    base = jnp.concatenate([wide[pl.ds(q, CHANNELS, stride=4), :] for q in range(4)], axis=1)
    weight = base[:, WEIGHT_SLOT : WEIGHT_SLOT + 1] + base[:, WEIGHT_SLOT + 1 : WEIGHT_SLOT + 2]
    weight = weight + base[:, WEIGHT_SLOT + 2 : WEIGHT_SLOT + 3]
    moved = jnp.concatenate([pltpu.roll(base, p, 1) if p else base for p in range(4)], axis=0)
    matrix[...] = moved.astype(jnp.bfloat16)
    upright = jnp.transpose(moved)
    for third in range(3):
        starts = [DEPTH * tap + 8 * third for tap in range(SPAN)]
        rows = [upright[at : at + 8] for at in starts] + [jnp.zeros((8, 4 * CHANNELS), f32)]
        turned[BAND * third : BAND * (third + 1), :] = jnp.concatenate(rows, axis=0).astype(jnp.bfloat16)
    inverse = 2.0 / jnp.sum(weight, axis=0, keepdims=True)
    twice = 2.0 * inverse
    def groups_of(n):
        return [2 * n, 2 * n + 1] if n < CHUNKS - 1 else [2 * n]

    def image_of(n):
        width = 128 * len(groups_of(n))
        cols = cols_ref[:, 256 * n : 256 * n + width]
        fields[n % 2, :, 0:width] = jnp.dot(matrix[...], cols, preferred_element_type=f32)

    def adjoint_of(n):
        groups = groups_of(n)
        width = 128 * len(groups)
        for p in range(4):
            field = fields[n % 2, CHANNELS * p : CHANNELS * (p + 1), 0:width]
            heavy = weight * field
            aerial = jnp.sum(heavy * field, axis=0, keepdims=True) * inverse
            resist = jax.nn.sigmoid(SLOPE * (aerial - LEVEL))
            spots = [4 * group + p for group in groups]
            target = jnp.concatenate([aux_ref[0, spot : spot + 1, :] for spot in spots], axis=1)
            scale = jnp.concatenate([aux_ref[1, spot : spot + 1, :] for spot in spots], axis=1)
            sense = scale * (resist - target) * resist * (1.0 - resist)
            for parity, spot in enumerate(spots):
                seen[spot : spot + 1, :] = resist[:, 128 * parity : 128 * parity + 128]
            value = (heavy * (twice * sense)).astype(jnp.bfloat16)
            adjoint[n % 2, CHANNELS * p : CHANNELS * (p + 1), 0:width] = value

    def spread_of(n):
        groups = groups_of(n)
        low, high = max(0, 2 - n), min(3, 11 - n)
        moved_in = adjoint[n % 2, :, 0 : 128 * len(groups)]
        spread = jnp.dot(turned[BAND * low : BAND * high, :], moved_in, preferred_element_type=f32)
        for third in range(low, high):
            tile = n + third
            for parity in range(len(groups)):
                if tile > 10 - parity:
                    continue
                at = BAND * (third - low)
                piece = spread[at : at + 8 * SPAN, 128 * parity : 128 * parity + 128]
                spot = tile - 2
                if third == 2:
                    sums[parity, spot, :, :] = piece
                elif third == 1:
                    sums[parity, spot, :, :] += piece
                else:
                    piece = piece + sums[parity, spot, :, :]
                    total = piece[0:8]
                    for tap in range(1, SPAN):
                        total = total + pltpu.roll(piece[8 * tap : 8 * tap + 8], tap, 1)
                    final[parity, 8 * spot : 8 * spot + 8, :] = total

    for step in range(CHUNKS + 2):
        if step < CHUNKS:
            image_of(step)
        if 0 <= step - 2:
            spread_of(step - 2)
        if 0 <= step - 1 < CHUNKS:
            adjoint_of(step - 1)
        if step == CHUNKS:
            resist_ref[...] = pltpu.roll(seen[10:74, :], 118, 1)[:, :OWN]
            resist_copy = pltpu.make_async_copy(resist_ref, resist_out, done.at[0])
            resist_copy.start()
    grad = final[0, 4:68, :] + final[1, 0:64, :]
    grad_ref[...] = pltpu.roll(grad, 108, 1)[:, :OWN]
    grad_copy = pltpu.make_async_copy(grad_ref, grad_out, done.at[1])
    grad_copy.start()
    resist_copy.wait()
    grad_copy.wait()


def image(taps, cols, aux):
    flops = 2 * 2 * 4 * CHANNELS * TAPS * 256 * CHUNKS
    return pl.pallas_call(
        image_kernel,
        out_shape=[
            jax.ShapeDtypeStruct((OWN, OWN), jnp.float32),
            jax.ShapeDtypeStruct((OWN, OWN), jnp.float32),
        ],
        in_specs=[pl.BlockSpec(memory_space=VMEM)] * 3,
        out_specs=[pl.BlockSpec(memory_space=pl.ANY)] * 2,
        scratch_shapes=[
            VMEM((OWN, OWN), jnp.float32),
            VMEM((OWN, OWN), jnp.float32),
            pltpu.SemaphoreType.DMA((2,)),
            VMEM((8 * SOURCES, 128), jnp.float32),
            VMEM((4 * CHANNELS, TAPS), jnp.bfloat16),
            VMEM((3 * BAND, 4 * CHANNELS), jnp.bfloat16),
            VMEM((2, 4 * CHANNELS, 256), jnp.float32),
            VMEM((2, 4 * CHANNELS, 256), jnp.bfloat16),
            VMEM((2, 9, 8 * SPAN, 128), jnp.float32),
            VMEM((88, 128), jnp.float32),
            VMEM((2, 72, 128), jnp.float32),
        ],
        cost_estimate=pl.CostEstimate(flops=flops, bytes_accessed=4 << 20, transcendentals=0),
        compiler_params=pltpu.CompilerParams(vmem_limit_bytes=20 << 20),
        name="image",
    )(taps, cols, aux)


def on_device(mask, target, kernels, source_weight, assign):
    tiles = lax.axis_size("tile")
    tile = lax.axis_index("tile").astype(jnp.int32).reshape(1)
    kern = lax.axis_index("kern").astype(jnp.int32).reshape(1)
    sent = pack(assign, kernels, source_weight)
    own, near, far = window(tile, kern, mask, target)
    taps = lax.all_to_all(sent, "kern", split_axis=0, concat_axis=0, tiled=True)

    def swapped(part, first):
        pairs = [(i, i + 1) for i in range(first, tiles - 1, 2)]
        return lax.ppermute(part, "tile", pairs + [(j, i) for i, j in pairs])

    far = swapped(far, 1)
    near = swapped(near, 0)
    cols, aux = columns(tile, kern, own, near, far)
    grad, resist = image(taps.reshape(SOURCES * 8, 128), cols, aux)
    return (grad, resist)


def solution(mesh):
    placed = (P("tile", None), P("tile", None), P("kern", None, None, None), P(), P("kern"))
    return jax.shard_map(
        on_device,
        mesh=mesh,
        in_specs=placed,
        out_specs=(P("tile", "kern"), P("tile", "kern")),
        check_vma=False,
    )
```

```python
import jax
import jax.numpy as jnp
from jax import lax
from jax.experimental import pallas as pl
from jax.experimental.pallas import tpu as pltpu
from jax.sharding import PartitionSpec as P

OWN = 64
SPAN = 21
HALF = 10
SOURCES = 32
CHANNELS = 2 * SOURCES
TILES = 16
DEPTH = 24
TAPS = 512
WEIGHT_SLOT = SPAN * DEPTH
CHUNKS = 11
BAND = 8 * SPAN + 8
SLOPE = 4.0
LEVEL = 0.6
VMEM = pltpu.VMEM


def in_hbm(array):
    return pltpu.with_memory_space_constraint(array, pltpu.HBM)


def pack_kernel(assign_ref, taps_ref, weight_ref, pack_ref, flat_ref):
    flat_ref[...] = jnp.zeros_like(flat_ref)
    for i in range(SPAN):
        flat_ref[2 * i : 2 * i + 2, 0:SPAN] = taps_ref[i].astype(jnp.float32)
    slot = lax.broadcasted_iota(jnp.int32, (128, TAPS), 1)
    low = DEPTH * lax.broadcasted_iota(jnp.int32, (128, TAPS), 0)
    spread = ((slot >= low) & (slot < low + DEPTH)).astype(jnp.float32).astype(jnp.bfloat16)
    wide = jnp.dot(flat_ref[...].astype(jnp.bfloat16), spread, preferred_element_type=jnp.float32)
    place = lax.broadcasted_iota(jnp.int32, wide.shape, 1).astype(jnp.float32)
    inner = place - DEPTH * jnp.floor((place + 0.5) * (1.0 / DEPTH))
    twice = 2.0 * inner
    row = lax.broadcasted_iota(jnp.int32, wide.shape, 0).astype(jnp.float32)
    index = lax.broadcasted_iota(jnp.int32, (1, SOURCES), 1)
    weight = jnp.sum(jnp.where(index == assign_ref[...], weight_ref[...], 0.0), axis=1, keepdims=True)
    lane = lax.broadcasted_iota(jnp.int32, (1, TAPS), 1)
    first = weight.astype(jnp.bfloat16).astype(jnp.float32)
    second = (weight - first).astype(jnp.bfloat16).astype(jnp.float32)
    third = weight - first - second
    rows = []
    for part in range(2):
        flat = jnp.sum(jnp.where(row == twice + part, wide, 0.0), axis=0, keepdims=True)
        for place, value in enumerate((first, second, third)):
            flat = jnp.where(lane == WEIGHT_SLOT + place, value, flat)
        rows += [flat[:, 128 * q : 128 * q + 128] for q in range(4)]
    pack_ref[...] = jnp.broadcast_to(jnp.concatenate(rows, axis=0).astype(jnp.bfloat16)[None], pack_ref.shape)


def pack(assign, kernels, source_weight):
    return pl.pallas_call(
        pack_kernel,
        out_shape=jax.ShapeDtypeStruct((SOURCES, 8, 128), jnp.bfloat16),
        in_specs=[pl.BlockSpec(memory_space=VMEM)] * 3,
        out_specs=pl.BlockSpec(memory_space=VMEM),
        scratch_shapes=[VMEM((48, 128), jnp.float32)],
        compiler_params=pltpu.CompilerParams(vmem_limit_bytes=8 << 20),
        name="pack",
    )(
        assign.reshape(1, 1),
        in_hbm(kernels.transpose(0, 2, 1, 3).reshape(SPAN, 2, SPAN)),
        in_hbm(source_weight.reshape(1, SOURCES)),
    )


def window_kernel(tile_ref, kern_ref, mask_a, mask_b, target_a, target_b, own_ref, near_ref, far_ref):
    kern = kern_ref[0]
    odd = lax.rem(kern, 2) == 1

    def cut(left, right, even_start, odd_start):
        left = jnp.where(kern > 0, left, 0.0)
        right = jnp.where(kern < SOURCES - 1, right, 0.0)
        both = jnp.concatenate([left, right], axis=1)
        even = pltpu.roll(both, 256 - even_start, 1)[:, :128]
        other = pltpu.roll(both, 256 - odd_start, 1)[:, :128]
        return jnp.where(odd, other, even).astype(jnp.bfloat16)

    mask = cut(mask_a[...], mask_b[...], 108, 44)
    target = cut(target_a[...].astype(jnp.float32), target_b[...].astype(jnp.float32), 118, 54)
    own_ref[0:64, :] = mask
    own_ref[64:128, :] = target
    even = lax.rem(tile_ref[0], 2) == 0
    near_ref[0:32, :] = jnp.where(even, mask[32:64], mask[0:32])
    near_ref[32:48, :] = jnp.where(even, target[48:64], target[0:16])
    far_ref[0:32, :] = jnp.where(even, mask[0:32], mask[32:64])
    far_ref[32:48, :] = jnp.where(even, target[0:16], target[48:64])


def window(tile, kern, mask, target):
    last = mask.shape[1] // 128 - 1

    def left(step, tile, kern):
        return (0, jnp.maximum(lax.div(kern[0] + 1, 2) - 1, 0))

    def right(step, tile, kern):
        return (0, jnp.minimum(lax.div(kern[0] + 1, 2), last))

    def zeros(rank):
        return lambda step, tile, kern: (0,) * rank

    mask, target = in_hbm(mask), in_hbm(target)
    return pl.pallas_call(
        window_kernel,
        grid_spec=pltpu.PrefetchScalarGridSpec(
            num_scalar_prefetch=2,
            grid=(1,),
            in_specs=[
                pl.BlockSpec((OWN, 128), left),
                pl.BlockSpec((OWN, 128), right),
                pl.BlockSpec((OWN, 128), left),
                pl.BlockSpec((OWN, 128), right),
            ],
            out_specs=[
                pl.BlockSpec((128, 128), zeros(2)),
                pl.BlockSpec((48, 128), zeros(2)),
                pl.BlockSpec((48, 128), zeros(2)),
            ],
        ),
        out_shape=[
            jax.ShapeDtypeStruct((128, 128), jnp.bfloat16),
            jax.ShapeDtypeStruct((48, 128), jnp.bfloat16),
            jax.ShapeDtypeStruct((48, 128), jnp.bfloat16),
        ],
        compiler_params=pltpu.CompilerParams(vmem_limit_bytes=8 << 20),
        name="window",
    )(
        tile,
        kern,
        mask,
        mask,
        target,
        target,
    )


def columns_kernel(tile_ref, kern_ref, own_ref, near_ref, far_ref, cols_ref, aux_ref, side, rows):
    f32 = jnp.float32
    even = lax.rem(tile_ref[0], 2) == 0
    near, far = near_ref[...].astype(f32), far_ref[...].astype(f32)
    side[0:48, :] = jnp.where(even, far, near)
    side[48:96, :] = jnp.where(even, near, far)
    rows[0:20, :] = side[12:32, :]
    rows[20:84, :] = own_ref[0:64, :].astype(f32)
    rows[84:104, :] = side[48:68, :]
    rows[104:112, :] = jnp.zeros((8, 128), f32)
    aux_ref[0, 0:10, :] = side[38:48, :]
    aux_ref[0, 10:74, :] = own_ref[64:128, :].astype(f32)
    aux_ref[0, 74:84, :] = side[80:90, :]
    aux_ref[0, 84:88, :] = jnp.zeros((4, 128), f32)
    row = lax.broadcasted_iota(jnp.int32, (88, 128), 0) + (OWN * tile_ref[0] - HALF)
    col = lax.broadcasted_iota(jnp.int32, (88, 128), 1) + (OWN * kern_ref[0] - HALF)
    inside = (row >= 0) & (row < OWN * TILES) & (col >= 0) & (col < OWN * SOURCES)
    aux_ref[1, :, :] = jnp.where(inside, 2.0 * SLOPE, 0.0)
    base = [rows[0:104, :], rows[4:108, :]]
    for first in range(0, SPAN, 2):
        turned = []
        for tap in (first, first + 1):
            if tap >= SPAN:
                turned.append(None)
            else:
                turned.append([pltpu.roll(b, 128 - tap, 1) if tap else b for b in base])
        for group in range(2 * CHUNKS):
            at = 8 * (group // 2)
            one = turned[0][group % 2][at : at + 24]
            if turned[1] is None:
                two = jnp.zeros((8, 128), f32)
            else:
                two = turned[1][group % 2][at : at + 24]
            block = jnp.concatenate([one, two], axis=0).astype(jnp.bfloat16)
            cols_ref[DEPTH * first : DEPTH * first + block.shape[0], 128 * group : 128 * group + 128] = block


def columns(tile, kern, own, near, far):
    return pl.pallas_call(
        columns_kernel,
        out_shape=[
            jax.ShapeDtypeStruct((TAPS, 256 * CHUNKS), jnp.bfloat16),
            jax.ShapeDtypeStruct((2, 88, 128), jnp.float32),
        ],
        in_specs=[pl.BlockSpec(memory_space=pltpu.SMEM)] * 2 + [pl.BlockSpec(memory_space=VMEM)] * 3,
        out_specs=[pl.BlockSpec(memory_space=VMEM)] * 2,
        scratch_shapes=[VMEM((96, 128), jnp.float32), VMEM((112, 128), jnp.float32)],
        compiler_params=pltpu.CompilerParams(vmem_limit_bytes=12 << 20),
        cost_estimate=pl.CostEstimate(flops=1 << 20, bytes_accessed=4 << 20, transcendentals=0),
        name="columns",
    )(tile, kern, own, near, far)


def image_kernel(taps_ref, cols_ref, aux_ref, grad_ref, resist_ref, wide, matrix, turned, fields, adjoint, sums, seen, final):
    f32 = jnp.float32
    wide[...] = taps_ref[...].astype(f32)
    base = jnp.concatenate([wide[pl.ds(q, CHANNELS, stride=4), :] for q in range(4)], axis=1)
    weight = base[:, WEIGHT_SLOT : WEIGHT_SLOT + 1] + base[:, WEIGHT_SLOT + 1 : WEIGHT_SLOT + 2]
    weight = weight + base[:, WEIGHT_SLOT + 2 : WEIGHT_SLOT + 3]
    moved = jnp.concatenate([pltpu.roll(base, p, 1) if p else base for p in range(4)], axis=0)
    matrix[...] = moved.astype(jnp.bfloat16)
    upright = jnp.transpose(moved)
    for third in range(3):
        starts = [DEPTH * tap + 8 * third for tap in range(SPAN)]
        rows = [upright[at : at + 8] for at in starts] + [jnp.zeros((8, 4 * CHANNELS), f32)]
        turned[BAND * third : BAND * (third + 1), :] = jnp.concatenate(rows, axis=0).astype(jnp.bfloat16)
    inverse = 2.0 / jnp.sum(weight, axis=0, keepdims=True)
    twice = 2.0 * inverse
    def groups_of(n):
        return [2 * n, 2 * n + 1] if n < CHUNKS - 1 else [2 * n]

    def image_of(n):
        width = 128 * len(groups_of(n))
        cols = cols_ref[:, 256 * n : 256 * n + width]
        fields[n % 2, :, 0:width] = jnp.dot(matrix[...], cols, preferred_element_type=f32)

    def adjoint_of(n):
        groups = groups_of(n)
        width = 128 * len(groups)
        for p in range(4):
            field = fields[n % 2, CHANNELS * p : CHANNELS * (p + 1), 0:width]
            heavy = weight * field
            aerial = jnp.sum(heavy * field, axis=0, keepdims=True) * inverse
            resist = jax.nn.sigmoid(SLOPE * (aerial - LEVEL))
            spots = [4 * group + p for group in groups]
            target = jnp.concatenate([aux_ref[0, spot : spot + 1, :] for spot in spots], axis=1)
            scale = jnp.concatenate([aux_ref[1, spot : spot + 1, :] for spot in spots], axis=1)
            sense = scale * (resist - target) * resist * (1.0 - resist)
            for parity, spot in enumerate(spots):
                seen[spot : spot + 1, :] = resist[:, 128 * parity : 128 * parity + 128]
            value = (heavy * (twice * sense)).astype(jnp.bfloat16)
            adjoint[n % 2, CHANNELS * p : CHANNELS * (p + 1), 0:width] = value

    def spread_of(n):
        groups = groups_of(n)
        low, high = max(0, 2 - n), min(3, 11 - n)
        moved_in = adjoint[n % 2, :, 0 : 128 * len(groups)]
        spread = jnp.dot(turned[BAND * low : BAND * high, :], moved_in, preferred_element_type=f32)
        for third in range(low, high):
            tile = n + third
            for parity in range(len(groups)):
                if tile > 10 - parity:
                    continue
                at = BAND * (third - low)
                piece = spread[at : at + 8 * SPAN, 128 * parity : 128 * parity + 128]
                spot = tile - 2
                if third == 2:
                    sums[parity, spot, :, :] = piece
                elif third == 1:
                    sums[parity, spot, :, :] += piece
                else:
                    piece = piece + sums[parity, spot, :, :]
                    total = piece[0:8]
                    for tap in range(1, SPAN):
                        total = total + pltpu.roll(piece[8 * tap : 8 * tap + 8], tap, 1)
                    final[parity, 8 * spot : 8 * spot + 8, :] = total

    for step in range(CHUNKS + 2):
        if step < CHUNKS:
            image_of(step)
        if 0 <= step - 2:
            spread_of(step - 2)
        if 0 <= step - 1 < CHUNKS:
            adjoint_of(step - 1)
    grad = final[0, 4:68, :] + final[1, 0:64, :]
    grad_ref[...] = pltpu.roll(grad, 108, 1)[:, :OWN]
    resist_ref[...] = pltpu.roll(seen[10:74, :], 118, 1)[:, :OWN]


def image(taps, cols, aux):
    flops = 2 * 2 * 4 * CHANNELS * TAPS * 256 * CHUNKS
    return pl.pallas_call(
        image_kernel,
        out_shape=[
            jax.ShapeDtypeStruct((OWN, OWN), jnp.float32),
            jax.ShapeDtypeStruct((OWN, OWN), jnp.float32),
        ],
        in_specs=[pl.BlockSpec(memory_space=VMEM)] * 3,
        out_specs=[pl.BlockSpec(memory_space=VMEM)] * 2,
        scratch_shapes=[
            VMEM((8 * SOURCES, 128), jnp.float32),
            VMEM((4 * CHANNELS, TAPS), jnp.bfloat16),
            VMEM((3 * BAND, 4 * CHANNELS), jnp.bfloat16),
            VMEM((2, 4 * CHANNELS, 256), jnp.float32),
            VMEM((2, 4 * CHANNELS, 256), jnp.bfloat16),
            VMEM((2, 9, 8 * SPAN, 128), jnp.float32),
            VMEM((88, 128), jnp.float32),
            VMEM((2, 72, 128), jnp.float32),
        ],
        cost_estimate=pl.CostEstimate(flops=flops, bytes_accessed=4 << 20, transcendentals=0),
        compiler_params=pltpu.CompilerParams(vmem_limit_bytes=20 << 20),
        name="image",
    )(taps, cols, aux)


def on_device(mask, target, kernels, source_weight, assign):
    tiles = lax.axis_size("tile")
    tile = lax.axis_index("tile").astype(jnp.int32).reshape(1)
    kern = lax.axis_index("kern").astype(jnp.int32).reshape(1)
    sent = pack(assign, kernels, source_weight)
    own, near, far = window(tile, kern, mask, target)
    taps = lax.all_to_all(sent, "kern", split_axis=0, concat_axis=0, tiled=True)

    def swapped(part, first):
        pairs = [(i, i + 1) for i in range(first, tiles - 1, 2)]
        return lax.ppermute(part, "tile", pairs + [(j, i) for i, j in pairs])

    far = swapped(far, 1)
    near = swapped(near, 0)
    cols, aux = columns(tile, kern, own, near, far)
    grad, resist = image(taps.reshape(SOURCES * 8, 128), cols, aux)
    return (grad, resist)


def solution(mesh):
    placed = (P("tile", None), P("tile", None), P("kern", None, None, None), P(), P("kern"))
    return jax.shard_map(
        on_device,
        mesh=mesh,
        in_specs=placed,
        out_specs=(P("tile", "kern"), P("tile", "kern")),
        check_vma=False,
    )
```
